32 devices in a mesh: row: 8 (over z, y), col: 4 (over x, core).
Axes of the slice: x: 2, y: 2, z: 4, core: 2. Of those that a mesh axis runs over, the one named last changes fastest.
Arguments:
- sub_field: float32 [65536, 128], P(('row', 'col')), may hold values from -2.4 to 2.4
- reluctivity: float32 [2, 65536, 128], P(None, ('row', 'col')), may hold values from 0.3 to 3
- stride: int32 [32], P(('row', 'col')), may hold values from 2 to 511
- counts: int32 [32, 8], P(('row', 'col')), may hold values from 1 to 32, as said below
- source_cell: int32 [32, 8, 32], P(('row', 'col')), may hold values from 0 to 2047
- target_row: int32 [8, 4, 8, 32], P('row', 'col'), may hold values from 0 to 2047
- lower_tiles: float32 [28, 2048, 2048], P(None, 'row', 'col'), may hold values from -0.046875 to 0.046875
- diag_inverse: float32 [8, 2048, 2048], P(None, 'col', 'row'), may hold values from -1 to 2, as said below
Outputs:
- solution: float32 [8, 4, 512, 128], P(None, 'col', 'row')
The draws below stay inside these ranges and needn't reach their ends.
Inputs may be any that keep to these rules, and one draw needn't show every extreme that they name: `counts`: every subdomain sends at least one contribution to every grid row; in every draw one grid row receives 32 contributions from every subdomain. `diag_inverse`: block i is the given inverse of the window's diagonal block i.
All inputs are finite; a program needn't handle non-finite values.
Results may differ from the reference program's by a relative error of at most 0.0003.
Values sent between devices are 32-bit elements; how exact they have to be, the bound alone decides.
A program may use at most 128 MiB of HBM per device.

```python
import math
import jax
import jax.numpy as jnp
from jax import lax

R = 128
TB = 256
WIN = 8
SC = 2048
CAP = 32
NB = 2048
CB = 512
PAIRS = 28
NSUB = 32
N_ROW = 8
N_COL = 4


def draw_counts(key, part):
    first_key, second_key = jax.random.split(key)
    hottest = jax.random.randint(first_key, (), 0, N_ROW)
    base_counts = jax.random.randint(second_key, (NSUB, N_ROW), 1, CAP + 1)
    columns = jnp.arange(N_ROW, dtype=jnp.int32)[None, :]
    return jnp.where(columns == hottest, CAP, base_counts).astype(jnp.int32)


def draw_diag_inverse(key, part):
    first_key, second_key = jax.random.split(key)
    rows = jnp.arange(NB, dtype=jnp.int32)[:, None]
    columns = jnp.arange(NB, dtype=jnp.int32)[None, :]
    identity = (rows == columns).astype(jnp.float32)
    spread = jax.random.normal(first_key, (WIN, NB, NB), jnp.float32) * (0.45 / NB ** 0.5)
    diagonal = jax.random.uniform(second_key, (WIN, NB), jnp.float32, 0.8, 1.2)
    return (spread + identity[None, :, :] * diagonal[:, :, None]).astype(jnp.float32)


def plant(entries, stream_key, smallest, top_value):
    longest = entries.shape.index(max(entries.shape))
    spots = []
    for shift in (0, 1):
        where = [jax.random.randint(jax.random.fold_in(stream_key, axis), (), 0, length) for axis, length in enumerate(entries.shape)]
        where[longest] = (where[longest] + shift) % entries.shape[longest]
        spots.append(tuple(where))
    return entries.at[spots[0]].set(smallest).at[spots[1]].set(top_value)


def shard_levels(key, shape, cuts, low, largest):
    def one(axis_at, shards_of):
        steps = jax.random.uniform(jax.random.fold_in(jax.random.fold_in(key, 6), axis_at), (shards_of,), jnp.float32, low / len(cuts), largest / len(cuts))
        return jnp.repeat(jnp.exp(steps), shape[axis_at] // shards_of).reshape((-1,) + (1,) * (len(shape) - axis_at - 1))

    level = one(*cuts[0])
    for cut in cuts[1:]:
        level = level * one(*cut)
    return level


def scatter_about(key, extent, scale, bound, shards=(), held_as=jnp.bfloat16):
    level = shard_levels(key, extent, shards, -0.22, 0.18) if shards else 1.0
    entries = jax.random.normal(key, extent, jnp.float32) * scale * level
    return jnp.minimum(jnp.maximum(entries, -bound), bound).astype(held_as)


def setup_inputs(seed: int = 0) -> dict:
    splits = jax.random.split(jax.random.key(seed), 9)
    return {
        "sub_field": scatter_about(splits[0], (NSUB * SC, R), 0.4, 2.4, ((0, 32),), jnp.float32),
        "reluctivity": jnp.clip(jnp.exp(math.log(3.0) - 2.3025851 * jax.random.uniform(splits[1], (2, NSUB * SC, R), jnp.float32) ** shard_levels(splits[1], (2, NSUB * SC, R), ((1, 32),), -0.2, 0.2)), 0.3, 3.0),
        "stride": plant(jax.random.randint(splits[2], (NSUB,), 2, SC // 4), jax.random.fold_in(splits[2], 1), 2, (SC // 4) - 1).astype(jnp.int32),
        "counts": draw_counts(jax.random.fold_in(splits[8], 71), 0),
        "source_cell": plant(jax.random.randint(splits[4], (NSUB, N_ROW, CAP), 0, SC), jax.random.fold_in(splits[4], 1), 0, SC - 1).astype(jnp.int32),
        "target_row": plant(jax.random.randint(splits[5], (N_ROW, N_COL, N_ROW, CAP), 0, WIN * TB), jax.random.fold_in(splits[5], 1), 0, (WIN * TB) - 1).astype(jnp.int32),
        "lower_tiles": scatter_about(splits[6], (PAIRS, NB, NB), (NB * WIN) ** -0.5, 0.046875, ((1, 8), (2, 4)), jnp.float32),
        "diag_inverse": draw_diag_inverse(jax.random.fold_in(splits[8], 71), 0),
    }


def sweep_subdomain(field, radial_nu, tangent_nu, stride_value):
    cell_index = jnp.arange(field.shape[0], dtype=jnp.int32)[:, None]
    radial_prev = jnp.where(cell_index >= stride_value, jnp.roll(field, stride_value, axis=0), 0.0)
    tangent_prev = jnp.where(cell_index >= 1, jnp.roll(field, 1, axis=0), 0.0)
    return radial_nu * (field - radial_prev) + tangent_nu * (field - tangent_prev)


def exact_dot(left, right):
    return jnp.dot(left, right, precision=lax.Precision.HIGHEST, preferred_element_type=jnp.float32)


def reference(sub_field, reluctivity, stride, counts, source_cell, target_row, lower_tiles, diag_inverse):
    subdomains = N_ROW * N_COL
    fields = sub_field.reshape(subdomains, SC, R)
    coefficients = reluctivity.reshape(2, subdomains, SC, R)
    swept = jax.vmap(sweep_subdomain)(fields, coefficients[0], coefficients[1], stride)
    owners = jnp.arange(subdomains, dtype=jnp.int32)[:, None, None]
    picked = swept[owners, source_cell]
    live = jnp.arange(CAP, dtype=jnp.int32)[None, None, :] < counts[:, :, None]
    picked = jnp.where(live[:, :, :, None], picked, 0.0)
    targets = jnp.transpose(target_row, (2, 1, 0, 3)).reshape(subdomains, N_ROW, CAP)
    grid_index = jnp.arange(N_ROW, dtype=jnp.int32)[None, :, None]
    global_row = (targets // TB) * NB + grid_index * TB + targets % TB
    rhs = jnp.zeros((WIN * NB, R), jnp.float32).at[global_row.reshape(-1)].add(picked.reshape(-1, R))
    rhs = rhs.reshape(WIN, NB, R)
    solved = []
    for row_block in range(WIN):
        residual = rhs[row_block]
        for earlier in range(row_block):
            residual = residual - exact_dot(lower_tiles[row_block * (row_block - 1) // 2 + earlier], solved[earlier])
        solved.append(exact_dot(diag_inverse[row_block], residual))
    return jnp.stack(solved).reshape(WIN, N_COL, CB, R)
```

```python
import functools

import jax
import jax.numpy as jnp
from jax import lax
from jax.experimental import pallas as pl
from jax.experimental.pallas import tpu as pltpu
from jax.sharding import PartitionSpec as P

MESH = pl.DeviceIdType.MESH
QUAD = 4
CORES = 2


def sweep_subdomain(field, radial_nu, tangent_nu, stride_value):
    cell_index = jnp.arange(field.shape[0], dtype=jnp.int32)[:, None]
    radial_prev = jnp.where(cell_index >= stride_value, jnp.roll(field, stride_value, axis=0), 0.0)
    tangent_prev = jnp.where(cell_index >= 1, jnp.roll(field, 1, axis=0), 0.0)
    return radial_nu * (field - radial_prev) + tangent_nu * (field - tangent_prev)


def pair_index(later_block, earlier_block):
    return later_block * (later_block - 1) // 2 + earlier_block


def halves(value, axis):
    high = value.astype(jnp.bfloat16)
    low = (value - high.astype(jnp.float32)).astype(jnp.bfloat16)
    return jnp.concatenate([high, low], axis=axis)


def split_product(left, right_halves):
    rows, rotor = left.shape[0], right_halves.shape[1] // 2
    full = jnp.dot(halves(left, 0), right_halves, preferred_element_type=jnp.float32)
    return (full[rows:, rotor:] + full[rows:, :rotor] + full[:rows, rotor:]) + full[:rows, :rotor]


def solve_kernel(
    n_row, n_col, rhs_ref, lower_hbm, diag_hbm, out_ref,
    lower, diag, acc, c1_in, c2_src, c2_in, res, part, a_in, b_src, b_in, ysh, yb,
    w_sem, d_sem, send_sem, recv_sem, c2_send, c2_recv,
):
    blocks = diag.shape[0]
    pairs = lower.shape[0]
    n_quads = n_row // QUAD
    n_x = n_col // CORES
    r = lax.axis_index("row")
    c = lax.axis_index("col")
    a, b = lax.rem(r, QUAD), lax.div(r, QUAD)
    core = lax.rem(c, CORES)
    core_peer = c + 1 - 2 * core
    x_peer = [lax.rem(c + CORES * s, n_col) for s in range(1, n_x)]
    a_off = [lax.rem(a + s, QUAD) for s in range(1, QUAD)]
    a_peer = [b * QUAD + o for o in a_off]
    b_off = [lax.rem(b + s, n_quads) for s in range(1, n_quads)]
    b_peer = [o * QUAD + a for o in b_off]

    def load_lower(k):
        return pltpu.make_async_copy(lower_hbm.at[k], lower.at[k], w_sem.at[k])

    def load_diag(k):
        return pltpu.make_async_copy(diag_hbm.at[k], diag.at[k], d_sem.at[k])

    for i in range(blocks):
        load_diag(i).start()
        for j in range(i):
            load_lower(pair_index(i, j)).start()

    barrier = pltpu.get_barrier_semaphore()
    pl.semaphore_signal(barrier, inc=1, device_id={"col": core_peer}, device_id_type=MESH)
    for p in x_peer:
        pl.semaphore_signal(barrier, inc=1, device_id={"col": p}, device_id_type=MESH)
    for p in a_peer + b_peer:
        pl.semaphore_signal(barrier, inc=1, device_id={"row": p}, device_id_type=MESH)
    acc[...] = rhs_ref[...]
    pl.semaphore_wait(barrier, 1 + len(x_peer) + len(a_peer) + len(b_peer))

    def remote(src, dst, k, device):
        return pltpu.make_async_remote_copy(
            src_ref=src, dst_ref=dst, send_sem=send_sem.at[k], recv_sem=recv_sem.at[k],
            device_id=device, device_id_type=MESH,
        )

    k_a = 2
    k_b = k_a + QUAD - 1
    k_bg = k_b + max(n_quads - 1, 0)
    k_ag = k_bg + max(n_quads - 1, 0)

    half_rows = acc.shape[2]
    rotor = acc.shape[3]

    def lower_step(i, j):
        k = pair_index(i, j)
        load_lower(k).wait()
        product = split_product(lower[k], yb[...])
        acc[i] = acc[i] - product.reshape(CORES, half_rows, rotor)

    def run(copies, work=None):
        for copy in copies:
            copy.start()
        if work is not None:
            work()
        for copy in copies:
            copy.wait()

    def step(i, carry):
        def deferred(*slots):
            def work():
                for t in slots:
                    @pl.when(jnp.logical_and(i > 0, i + 1 + t < blocks))
                    def _():
                        lower_step(i + 1 + t, i - 1)
            return work

        @pl.when(i > 0)
        def _():
            lower_step(i, i - 1)

        run([remote(acc.at[i, 1 - core], c1_in, 0, {"col": core_peer})])
        c2_src[...] = acc[i, core] + c1_in[...]
        parity = lax.rem(i, 2)
        run(
            [
                pltpu.make_async_remote_copy(
                    src_ref=c2_src, dst_ref=c2_in.at[parity, s], send_sem=c2_send.at[parity, s],
                    recv_sem=c2_recv.at[parity, s], device_id={"col": p}, device_id_type=MESH,
                )
                for s, p in enumerate(x_peer)
            ],
            deferred(0),
        )
        total = c2_src[...]
        for s in range(n_x - 1):
            total = total + c2_in[parity, s]
        res[core] = total
        load_diag(i).wait()
        run([remote(res.at[core], res.at[core], 1, {"col": core_peer})])

        residual = res[...].reshape(CORES * half_rows, rotor)
        part[...] = split_product(diag[i], halves(residual, 1)).reshape(part.shape)
        run(
            [
                remote(part.at[:, o], a_in.at[s], k_a + s, {"row": p})
                for s, (o, p) in enumerate(zip(a_off, a_peer))
            ],
            deferred(1, 2),
        )
        total = part[:, a]
        for s in range(QUAD - 1):
            total = total + a_in[s]
        b_src[...] = total
        run(
            [
                remote(b_src.at[o], b_in.at[s], k_b + s, {"row": p})
                for s, (o, p) in enumerate(zip(b_off, b_peer))
            ],
            deferred(3),
        )
        total = b_src[b]
        for s in range(n_quads - 1):
            total = total + b_in[s]
        ysh[b, a] = total
        out_ref[i] = total

        @pl.when(i < blocks - 1)
        def _():
            run(
                [
                    remote(ysh.at[b, a], ysh.at[b, a], k_bg + s, {"row": p})
                    for s, p in enumerate(b_peer)
                ],
                deferred(4),
            )
            run(
                [
                    remote(ysh.at[:, a], ysh.at[:, a], k_ag + s, {"row": p})
                    for s, p in enumerate(a_peer)
                ],
                deferred(5),
            )
            yb[...] = halves(ysh[...].reshape(yb.shape[0], rotor), 1)

        return carry

    lax.fori_loop(0, blocks, step, 0)


def solve(interface, lower_tiles, diag_inverse):
    n_row, n_col = lax.axis_size("row"), lax.axis_size("col")
    blocks, tile_rows, rotor = interface.shape
    pairs = lower_tiles.shape[0]
    share = diag_inverse.shape[1]
    piece = share // n_row
    quads = n_row // QUAD
    n_x = n_col // CORES
    half = tile_rows // CORES
    f32 = jnp.float32
    copies = 2 + 2 * (QUAD - 1) + 2 * (quads - 1)
    vmem = pl.BlockSpec(memory_space=pltpu.VMEM)
    hbm = pl.BlockSpec(memory_space=pl.ANY)
    return pl.pallas_call(
        functools.partial(solve_kernel, n_row, n_col),
        out_shape=jax.ShapeDtypeStruct((blocks, piece, rotor), f32),
        in_specs=[vmem, hbm, hbm],
        out_specs=vmem,
        scratch_shapes=[
            pltpu.VMEM(lower_tiles.shape, f32),
            pltpu.VMEM(diag_inverse.shape, f32),
            pltpu.VMEM((blocks, CORES, half, rotor), f32),
            pltpu.VMEM((half, rotor), f32),
            pltpu.VMEM((half, rotor), f32),
            pltpu.VMEM((2, n_x - 1, half, rotor), f32),
            pltpu.VMEM((CORES, half, rotor), f32),
            pltpu.VMEM((quads, QUAD, piece, rotor), f32),
            pltpu.VMEM((QUAD - 1, quads, piece, rotor), f32),
            pltpu.VMEM((quads, piece, rotor), f32),
            pltpu.VMEM((quads - 1, piece, rotor), f32),
            pltpu.VMEM((quads, QUAD, piece, rotor), f32),
            pltpu.VMEM((share, 2 * rotor), jnp.bfloat16),
            pltpu.SemaphoreType.DMA((pairs,)),
            pltpu.SemaphoreType.DMA((blocks,)),
            pltpu.SemaphoreType.DMA((copies,)),
            pltpu.SemaphoreType.DMA((copies,)),
            pltpu.SemaphoreType.DMA((2, n_x - 1)),
            pltpu.SemaphoreType.DMA((2, n_x - 1)),
        ],
        compiler_params=pltpu.CompilerParams(
            collective_id=0, has_side_effects=True, vmem_limit_bytes=48 * 1024 * 1024
        ),
    )(interface.reshape(blocks, CORES, half, rotor), lower_tiles, diag_inverse)


def per_device(
    sub_field, reluctivity, stride, counts, source_cell, target_row, lower_tiles, diag_inverse
):
    blocks = diag_inverse.shape[0]
    tile_rows = lower_tiles.shape[1]
    rotor = sub_field.shape[1]
    swept = sweep_subdomain(sub_field, reluctivity[0], reluctivity[1], stride[0])
    picked = swept[source_cell[0]]
    slots = source_cell.shape[2]
    live = jnp.arange(slots, dtype=jnp.int32)[None, :] < counts[0][:, None]
    picked = jnp.where(live[:, :, None], picked, 0.0)
    received = lax.all_to_all(picked, "row", split_axis=0, concat_axis=0, tiled=True)
    targets = target_row[0, 0].reshape(-1)
    interface = (
        jnp.zeros((blocks * tile_rows, rotor), jnp.float32)
        .at[targets]
        .add(received.reshape(-1, rotor))
    )
    interface = interface.reshape(blocks, tile_rows, rotor)
    return solve(interface, lower_tiles, diag_inverse)[:, None]


def solution(mesh):
    placed = (
        P(("row", "col"), None),
        P(None, ("row", "col"), None),
        P(("row", "col")),
        P(("row", "col"), None),
        P(("row", "col"), None, None),
        P("row", "col", None, None),
        P(None, "row", "col"),
        P(None, "col", "row"),
    )
    return jax.shard_map(
        per_device,
        mesh=mesh,
        in_specs=placed,
        out_specs=P(None, "col", "row", None),
        check_vma=False,
    )
```

```python
import functools

import jax
import jax.numpy as jnp
from jax import lax
from jax.experimental import pallas as pl
from jax.experimental.pallas import tpu as pltpu
from jax.sharding import PartitionSpec as P

MESH = pl.DeviceIdType.MESH
QUAD = 4
CORES = 2


def sweep_subdomain(field, radial_nu, tangent_nu, stride_value):
    cell_index = jnp.arange(field.shape[0], dtype=jnp.int32)[:, None]
    radial_prev = jnp.where(cell_index >= stride_value, jnp.roll(field, stride_value, axis=0), 0.0)
    tangent_prev = jnp.where(cell_index >= 1, jnp.roll(field, 1, axis=0), 0.0)
    return radial_nu * (field - radial_prev) + tangent_nu * (field - tangent_prev)


def pair_index(later_block, earlier_block):
    return later_block * (later_block - 1) // 2 + earlier_block


def halves(value, axis):
    high = value.astype(jnp.bfloat16)
    low = (value - high.astype(jnp.float32)).astype(jnp.bfloat16)
    return jnp.concatenate([high, low], axis=axis)


def split_product(left, right_halves):
    rows, rotor = left.shape[0], right_halves.shape[1] // 2
    full = jnp.dot(halves(left, 0), right_halves, preferred_element_type=jnp.float32)
    return (full[rows:, rotor:] + full[rows:, :rotor] + full[:rows, rotor:]) + full[:rows, :rotor]


def solve_kernel(
    n_row, n_col, rhs_ref, lower_hbm, diag_hbm, out_ref,
    lower, diag, acc, c1_in, c2_src, c2_in, res, part, a_in, b_src, b_in, ysh, yb,
    w_sem, d_sem, c1_sems, c2_sems, c3_sems, a_sems, b_sems, g_sems,
):
    blocks = diag.shape[0]
    n_quads = n_row // QUAD
    n_x = n_col // CORES
    chunks, chunk_rows, rotor = acc.shape[2:]
    half_rows = chunks * chunk_rows
    chunk_share = diag.shape[1] // n_quads
    r = lax.axis_index("row")
    c = lax.axis_index("col")
    a, b = lax.rem(r, QUAD), lax.div(r, QUAD)
    core = lax.rem(c, CORES)
    other = 1 - core
    core_peer = {"col": c + 1 - 2 * core}
    x_peer = [{"col": lax.rem(c + CORES * s, n_col)} for s in range(1, n_x)]
    a_off = [lax.rem(a + s, QUAD) for s in range(1, QUAD)]
    a_peer = [{"row": b * QUAD + o} for o in a_off]
    b_peer = [{"row": lax.rem(b + s, n_quads) * QUAD + a} for s in range(1, n_quads)]
    peers = [core_peer] + x_peer + a_peer + b_peer

    def load_lower(k):
        return pltpu.make_async_copy(lower_hbm.at[k], lower.at[k], w_sem.at[k])

    def load_diag(k):
        return pltpu.make_async_copy(diag_hbm.at[k], diag.at[k], d_sem.at[k])

    for i in range(blocks):
        load_diag(i).start()
        for j in range(i):
            load_lower(pair_index(i, j)).start()

    barrier = pltpu.get_barrier_semaphore()
    for p in peers:
        pl.semaphore_signal(barrier, inc=1, device_id=p, device_id_type=MESH)
    acc[...] = rhs_ref[...]
    pl.semaphore_wait(barrier, len(peers))

    def remote(src, dst, sems, at, device):
        copy = pltpu.make_async_remote_copy(
            src_ref=src, dst_ref=dst, send_sem=sems.at[(0,) + at], recv_sem=sems.at[(1,) + at],
            device_id=device, device_id_type=MESH,
        )
        copy.start()
        return copy

    def finish(copies):
        for copy in copies:
            copy.wait()

    def lower_step(i, j):
        k = pair_index(i, j)
        load_lower(k).wait()
        product = split_product(lower[k], yb[...])
        acc[i] = acc[i] - product.reshape(acc.shape[1:])

    def lower_half(i, side):
        start = pl.multiple_of(side * half_rows, half_rows)
        product = split_product(lower[pair_index(i, i - 1), pl.ds(start, half_rows)], yb[...])
        acc[i, side] = acc[i, side] - product.reshape(acc.shape[2:])

    def step(i, carry):
        parity = lax.rem(i, 2)

        def deferred(*slots):
            for t in slots:
                @pl.when(jnp.logical_and(i > 0, i + 1 + t < blocks))
                def _():
                    lower_step(i + 1 + t, i - 1)

        @pl.when(i > 0)
        def _():
            load_lower(pair_index(i, i - 1)).wait()
            lower_half(i, other)

        c1 = [
            remote(acc.at[i, other, q], c1_in.at[q], c1_sems, (q,), core_peer)
            for q in range(chunks)
        ]

        @pl.when(i > 0)
        def _():
            lower_half(i, core)

        c2 = []
        for q in range(chunks):
            c1[q].wait()
            c2_src[q] = acc[i, core, q] + c1_in[q]
            c2.append([
                remote(c2_src.at[q], c2_in.at[parity, q, s], c2_sems, (parity, q, s), p)
                for s, p in enumerate(x_peer)
            ])
        deferred(0)
        c3 = []
        for q in range(chunks):
            finish(c2[q])
            total = c2_src[q]
            for s in range(n_x - 1):
                total = total + c2_in[parity, q, s]
            res[core, q] = total
            c3.append(remote(res.at[core, q], res.at[core, q], c3_sems, (q,), core_peer))
        load_diag(i).wait()
        finish(c3)

        residual = halves(res[...].reshape(CORES * half_rows, rotor), 1)
        a_copies = []
        for h in range(n_quads):
            rows = diag[i, h * chunk_share:(h + 1) * chunk_share]
            part[h] = split_product(rows, residual).reshape(part.shape[1:])
            a_copies.append([
                remote(part.at[h, o], a_in.at[h, s], a_sems, (h, s), p)
                for s, (o, p) in enumerate(zip(a_off, a_peer))
            ])
        deferred(1, 2)
        b_copies = []
        for h in range(n_quads):
            finish(a_copies[h])
            total = part[h, a]
            for s in range(QUAD - 1):
                total = total + a_in[h, s]
            b_src[h] = total
            b_copies.append([
                remote(b_src.at[h], b_in.at[parity, h, s], b_sems, (parity, h, s), p)
                for s, p in enumerate(b_peer)
            ])
        deferred(3)

        def across(h):
            finish(b_copies[h])
            total = b_src[h]
            for s in range(n_quads - 1):
                total = total + b_in[parity, h, s]
            ysh[h, a] = total

        @pl.when(i < blocks - 1)
        def _():
            back = []
            for h in range(n_quads):
                across(h)
                back.append([
                    remote(ysh.at[h, a], ysh.at[h, a], g_sems, (h, s), p)
                    for s, p in enumerate(a_peer)
                ])
            deferred(4, 5)
            for h in range(n_quads):
                finish(back[h])
            yb[...] = halves(ysh[...].reshape(yb.shape[0], rotor), 1)

        @pl.when(i == blocks - 1)
        def _():
            for h in range(n_quads):
                across(h)

        out_ref[i] = ysh[b, a]
        return carry

    lax.fori_loop(0, blocks, step, 0)


def solve(interface, lower_tiles, diag_inverse):
    n_row, n_col = lax.axis_size("row"), lax.axis_size("col")
    blocks, tile_rows, rotor = interface.shape
    pairs = lower_tiles.shape[0]
    share = diag_inverse.shape[1]
    piece = share // n_row
    quads = n_row // QUAD
    n_x = n_col // CORES
    chunks = 2
    col_chunk = (chunks, tile_rows // CORES // chunks, rotor)
    f32 = jnp.float32
    vmem = pl.BlockSpec(memory_space=pltpu.VMEM)
    hbm = pl.BlockSpec(memory_space=pl.ANY)
    dma = pltpu.SemaphoreType.DMA
    return pl.pallas_call(
        functools.partial(solve_kernel, n_row, n_col),
        out_shape=jax.ShapeDtypeStruct((blocks, piece, rotor), f32),
        in_specs=[vmem, hbm, hbm],
        out_specs=vmem,
        scratch_shapes=[
            pltpu.VMEM(lower_tiles.shape, f32),
            pltpu.VMEM(diag_inverse.shape, f32),
            pltpu.VMEM((blocks, CORES) + col_chunk, f32),
            pltpu.VMEM(col_chunk, f32),
            pltpu.VMEM(col_chunk, f32),
            pltpu.VMEM((2, chunks, n_x - 1) + col_chunk[1:], f32),
            pltpu.VMEM((CORES,) + col_chunk, f32),
            pltpu.VMEM((quads, QUAD, piece, rotor), f32),
            pltpu.VMEM((quads, QUAD - 1, piece, rotor), f32),
            pltpu.VMEM((quads, piece, rotor), f32),
            pltpu.VMEM((2, quads, quads - 1, piece, rotor), f32),
            pltpu.VMEM((quads, QUAD, piece, rotor), f32),
            pltpu.VMEM((share, 2 * rotor), jnp.bfloat16),
            dma((pairs,)),
            dma((blocks,)),
            dma((2, chunks)),
            dma((2, 2, chunks, n_x - 1)),
            dma((2, chunks)),
            dma((2, quads, QUAD - 1)),
            dma((2, 2, quads, quads - 1)),
            dma((2, quads, QUAD - 1)),
        ],
        compiler_params=pltpu.CompilerParams(
            collective_id=0, has_side_effects=True, vmem_limit_bytes=48 * 1024 * 1024
        ),
    )(interface.reshape((blocks, CORES) + col_chunk), lower_tiles, diag_inverse)


def per_device(
    sub_field, reluctivity, stride, counts, source_cell, target_row, lower_tiles, diag_inverse
):
    blocks = diag_inverse.shape[0]
    tile_rows = lower_tiles.shape[1]
    rotor = sub_field.shape[1]
    swept = sweep_subdomain(sub_field, reluctivity[0], reluctivity[1], stride[0])
    picked = swept[source_cell[0]]
    slots = source_cell.shape[2]
    live = jnp.arange(slots, dtype=jnp.int32)[None, :] < counts[0][:, None]
    picked = jnp.where(live[:, :, None], picked, 0.0)
    received = lax.all_to_all(picked, "row", split_axis=0, concat_axis=0, tiled=True)
    targets = target_row[0, 0].reshape(-1)
    interface = (
        jnp.zeros((blocks * tile_rows, rotor), jnp.float32)
        .at[targets]
        .add(received.reshape(-1, rotor))
    )
    interface = interface.reshape(blocks, tile_rows, rotor)
    return solve(interface, lower_tiles, diag_inverse)[:, None]


def solution(mesh):
    placed = (
        P(("row", "col"), None),
        P(None, ("row", "col"), None),
        P(("row", "col")),
        P(("row", "col"), None),
        P(("row", "col"), None, None),
        P("row", "col", None, None),
        P(None, "row", "col"),
        P(None, "col", "row"),
    )
    return jax.shard_map(
        per_device,
        mesh=mesh,
        in_specs=placed,
        out_specs=P(None, "col", "row", None),
        check_vma=False,
    )
```

```python
import functools

import jax
import jax.numpy as jnp
from jax import lax
from jax.experimental import pallas as pl
from jax.experimental.pallas import tpu as pltpu
from jax.sharding import PartitionSpec as P

MESH = pl.DeviceIdType.MESH
QUAD = 4
CORES = 2
PICKS = 8


def pair_index(later_block, earlier_block):
    return later_block * (later_block - 1) // 2 + earlier_block


def halves(value, axis):
    high = value.astype(jnp.bfloat16)
    low = (value - high.astype(jnp.float32)).astype(jnp.bfloat16)
    return jnp.concatenate([high, low], axis=axis)


def split_product(left, right_halves):
    rows, rotor = left.shape[0], right_halves.shape[1] // 2
    full = jnp.dot(halves(left, 0), right_halves, preferred_element_type=jnp.float32)
    return (full[rows:, rotor:] + full[rows:, :rotor] + full[:rows, rotor:]) + full[:rows, :rotor]


def solve_kernel(
    n_row, n_col, stride, counts, source, target_ref, field_hbm, nu_hbm, lower_hbm, diag_hbm,
    out_ref, field, nu, picked, received, arrived, lower, diag, acc, c1_in, c2_src, c2_in, res, part, a_in, b_src, b_in, ysh, yb,
    f_sem, p_sems, w_sem, d_sem, c1_sems, c2_sems, c3_sems, a_sems, b_sems, g_sems,
):
    blocks = diag.shape[0]
    n_quads = n_row // QUAD
    n_x = n_col // CORES
    chunks, chunk_rows, rotor = acc.shape[2:]
    half_rows = chunks * chunk_rows
    chunk_share = diag.shape[1] // n_quads
    r = lax.axis_index("row")
    c = lax.axis_index("col")
    a, b = lax.rem(r, QUAD), lax.div(r, QUAD)
    core = lax.rem(c, CORES)
    other = 1 - core
    core_peer = {"col": c + 1 - 2 * core}
    x_peer = [{"col": lax.rem(c + CORES * s, n_col)} for s in range(1, n_x)]
    a_off = [lax.rem(a + s, QUAD) for s in range(1, QUAD)]
    a_peer = [{"row": b * QUAD + o} for o in a_off]
    b_peer = [{"row": lax.rem(b + s, n_quads) * QUAD + a} for s in range(1, n_quads)]
    row_at = [lax.rem(r + s, n_row) for s in range(n_row)]
    peers = [core_peer] + x_peer + [{"row": g} for g in row_at[1:]]
    slots = source.shape[2]

    def load_lower(k):
        return pltpu.make_async_copy(lower_hbm.at[k], lower.at[k], w_sem.at[k])

    def load_diag(k):
        return pltpu.make_async_copy(diag_hbm.at[k], diag.at[k], d_sem.at[k])

    def load_cells():
        return (
            pltpu.make_async_copy(field_hbm, field, f_sem.at[0]),
            pltpu.make_async_copy(nu_hbm, nu, f_sem.at[1]),
        )

    for copy in load_cells():
        copy.start()
    barrier = pltpu.get_barrier_semaphore()
    for p in peers:
        pl.semaphore_signal(barrier, inc=1, device_id=p, device_id_type=MESH)

    def remote(src, dst, sems, at, device):
        copy = pltpu.make_async_remote_copy(
            src_ref=src, dst_ref=dst, send_sem=sems.at[(0,) + at], recv_sem=sems.at[(1,) + at],
            device_id=device, device_id_type=MESH,
        )
        copy.start()
        return copy

    def finish(copies):
        for copy in copies:
            copy.wait()

    band = stride[0]

    def pick(s):
        g = row_at[s]
        live_slots = counts[0, g]

        def group(k8, carry):
            for u in range(PICKS):
                k = k8 * PICKS + u
                m = source[0, g, k]
                here = field[pl.ds(m, 1), :]
                radial = field[pl.ds(jnp.maximum(m - band, 0), 1), :]
                tangent = field[pl.ds(jnp.maximum(m - 1, 0), 1), :]
                has_radial = jnp.where(m >= band, 1.0, 0.0)
                has_tangent = jnp.where(m >= 1, 1.0, 0.0)
                live = jnp.where(k < live_slots, 1.0, 0.0)
                swept = nu[0, pl.ds(m, 1), :] * (here - radial * has_radial) + nu[
                    1, pl.ds(m, 1), :
                ] * (here - tangent * has_tangent)
                picked[s, pl.ds(k, 1), :] = swept * live
            return carry

        lax.fori_loop(0, slots // PICKS, group, 0)

    for copy in load_cells():
        copy.wait()
    for i in range(blocks):
        load_diag(i).start()
        for j in range(i):
            load_lower(pair_index(i, j)).start()
    sent = []
    for s in range(1, n_row):
        pick(s)
        if s == 1:
            pl.semaphore_wait(barrier, len(peers))
        sent.append(remote(picked.at[s], received.at[r], p_sems, (s - 1,), {"row": row_at[s]}))
    pick(0)
    received[r] = picked[0]
    finish(sent)
    arrived[...] = halves(received[...].reshape(arrived.shape[0], rotor), 1)

    def place(i):
        rows = CORES * half_rows
        here = lax.broadcasted_iota(jnp.int32, (rows, arrived.shape[0]), 0) + i * rows
        chosen = jnp.where(here == target_ref[...], 1.0, 0.0).astype(jnp.bfloat16)
        full = jnp.dot(chosen, arrived[...], preferred_element_type=jnp.float32)
        acc[i] = (full[:, :rotor] + full[:, rotor:]).reshape(acc.shape[1:])

    place(0)

    def lower_step(i, j):
        k = pair_index(i, j)
        load_lower(k).wait()
        product = split_product(lower[k], yb[...])
        acc[i] = acc[i] - product.reshape(acc.shape[1:])

    def lower_half(i, side):
        start = pl.multiple_of(side * half_rows, half_rows)
        product = split_product(lower[pair_index(i, i - 1), pl.ds(start, half_rows)], yb[...])
        acc[i, side] = acc[i, side] - product.reshape(acc.shape[2:])

    def step(i, carry):
        parity = lax.rem(i, 2)

        def deferred(*turns):
            for t in turns:
                @pl.when(jnp.logical_and(i > 0, i + 1 + t < blocks))
                def _():
                    lower_step(i + 1 + t, i - 1)

            @pl.when(i == 0)
            def _():
                for t in turns:
                    if 1 + t < blocks:
                        place(1 + t)

        @pl.when(i > 0)
        def _():
            load_lower(pair_index(i, i - 1)).wait()
            lower_half(i, other)

        c1 = [
            remote(acc.at[i, other, q], c1_in.at[q], c1_sems, (q,), core_peer)
            for q in range(chunks)
        ]

        @pl.when(i > 0)
        def _():
            lower_half(i, core)

        c2 = []
        for q in range(chunks):
            c1[q].wait()
            c2_src[q] = acc[i, core, q] + c1_in[q]
            c2.append([
                remote(c2_src.at[q], c2_in.at[parity, q, s], c2_sems, (parity, q, s), p)
                for s, p in enumerate(x_peer)
            ])
        deferred(0)
        c3 = []
        for q in range(chunks):
            finish(c2[q])
            total = c2_src[q]
            for s in range(n_x - 1):
                total = total + c2_in[parity, q, s]
            res[core, q] = total
            c3.append(remote(res.at[core, q], res.at[core, q], c3_sems, (q,), core_peer))
        load_diag(i).wait()
        finish(c3)

        residual = halves(res[...].reshape(CORES * half_rows, rotor), 1)
        a_copies = []
        for h in range(n_quads):
            rows = diag[i, h * chunk_share:(h + 1) * chunk_share]
            part[h] = split_product(rows, residual).reshape(part.shape[1:])
            a_copies.append([
                remote(part.at[h, o], a_in.at[h, s], a_sems, (h, s), p)
                for s, (o, p) in enumerate(zip(a_off, a_peer))
            ])
        deferred(1, 2)
        b_copies = []
        for h in range(n_quads):
            finish(a_copies[h])
            total = part[h, a]
            for s in range(QUAD - 1):
                total = total + a_in[h, s]
            b_src[h] = total
            b_copies.append([
                remote(b_src.at[h], b_in.at[parity, h, s], b_sems, (parity, h, s), p)
                for s, p in enumerate(b_peer)
            ])
        deferred(3)

        def across(h):
            finish(b_copies[h])
            total = b_src[h]
            for s in range(n_quads - 1):
                total = total + b_in[parity, h, s]
            ysh[h, a] = total

        @pl.when(i < blocks - 1)
        def _():
            back = []
            for h in range(n_quads):
                across(h)
                back.append([
                    remote(ysh.at[h, a], ysh.at[h, a], g_sems, (h, s), p)
                    for s, p in enumerate(a_peer)
                ])
            deferred(*range(4, blocks - 1))
            for h in range(n_quads):
                finish(back[h])
            yb[...] = halves(ysh[...].reshape(yb.shape[0], rotor), 1)

        @pl.when(i == blocks - 1)
        def _():
            for h in range(n_quads):
                across(h)

        out_ref[i] = ysh[b, a]
        return carry

    lax.fori_loop(0, blocks, step, 0)


def per_device(
    sub_field, reluctivity, stride, counts, source_cell, target_row, lower_tiles, diag_inverse
):
    n_row, n_col = lax.axis_size("row"), lax.axis_size("col")
    blocks, tile_rows, rotor = diag_inverse.shape[0], lower_tiles.shape[1], sub_field.shape[1]
    cap = source_cell.shape[2]
    pairs = lower_tiles.shape[0]
    share = diag_inverse.shape[1]
    piece = share // n_row
    quads = n_row // QUAD
    n_x = n_col // CORES
    chunks = 2
    col_chunk = (chunks, tile_rows // CORES // chunks, rotor)
    f32 = jnp.float32
    vmem = pl.BlockSpec(memory_space=pltpu.VMEM)
    smem = pl.BlockSpec(memory_space=pltpu.SMEM)
    hbm = pl.BlockSpec(memory_space=pl.ANY)
    dma = pltpu.SemaphoreType.DMA
    pieces = pl.pallas_call(
        functools.partial(solve_kernel, n_row, n_col),
        out_shape=jax.ShapeDtypeStruct((blocks, piece, rotor), f32),
        in_specs=[smem, smem, smem, vmem, hbm, hbm, hbm, hbm],
        out_specs=vmem,
        scratch_shapes=[
            pltpu.VMEM(sub_field.shape, f32),
            pltpu.VMEM(reluctivity.shape, f32),
            pltpu.VMEM((n_row, cap, rotor), f32),
            pltpu.VMEM((n_row, cap, rotor), f32),
            pltpu.VMEM((n_row * cap, 2 * rotor), jnp.bfloat16),
            pltpu.VMEM(lower_tiles.shape, f32),
            pltpu.VMEM(diag_inverse.shape, f32),
            pltpu.VMEM((blocks, CORES) + col_chunk, f32),
            pltpu.VMEM(col_chunk, f32),
            pltpu.VMEM(col_chunk, f32),
            pltpu.VMEM((2, chunks, n_x - 1) + col_chunk[1:], f32),
            pltpu.VMEM((CORES,) + col_chunk, f32),
            pltpu.VMEM((quads, QUAD, piece, rotor), f32),
            pltpu.VMEM((quads, QUAD - 1, piece, rotor), f32),
            pltpu.VMEM((quads, piece, rotor), f32),
            pltpu.VMEM((2, quads, quads - 1, piece, rotor), f32),
            pltpu.VMEM((quads, QUAD, piece, rotor), f32),
            pltpu.VMEM((share, 2 * rotor), jnp.bfloat16),
            dma((2,)),
            dma((2, n_row - 1)),
            dma((pairs,)),
            dma((blocks,)),
            dma((2, chunks)),
            dma((2, 2, chunks, n_x - 1)),
            dma((2, chunks)),
            dma((2, quads, QUAD - 1)),
            dma((2, 2, quads, quads - 1)),
            dma((2, quads, QUAD - 1)),
        ],
        compiler_params=pltpu.CompilerParams(
            collective_id=0, has_side_effects=True, vmem_limit_bytes=48 * 1024 * 1024
        ),
    )(
        stride, counts, source_cell, target_row.reshape(1, n_row * cap),
        sub_field, reluctivity, lower_tiles, diag_inverse,
    )
    return pieces[:, None]


def solution(mesh):
    placed = (
        P(("row", "col"), None),
        P(None, ("row", "col"), None),
        P(("row", "col")),
        P(("row", "col"), None),
        P(("row", "col"), None, None),
        P("row", "col", None, None),
        P(None, "row", "col"),
        P(None, "col", "row"),
    )
    return jax.shard_map(
        per_device,
        mesh=mesh,
        in_specs=placed,
        out_specs=P(None, "col", "row", None),
        check_vma=False,
    )
```

```python
import functools

import jax
import jax.numpy as jnp
from jax import lax
from jax.experimental import pallas as pl
from jax.experimental.pallas import tpu as pltpu
from jax.sharding import PartitionSpec as P

MESH = pl.DeviceIdType.MESH
QUAD = 4
CORES = 2
PICKS = 8
SPLIT = 2


def pair_index(later_block, earlier_block):
    return later_block * (later_block - 1) // 2 + earlier_block


def halves(value, axis):
    high = value.astype(jnp.bfloat16)
    low = (value - high.astype(jnp.float32)).astype(jnp.bfloat16)
    return jnp.concatenate([high, low], axis=axis)


def split_product(left, right_halves):
    rows, rotor = left.shape[0], right_halves.shape[1] // 2
    full = jnp.dot(halves(left, 0), right_halves, preferred_element_type=jnp.float32)
    return (full[rows:, rotor:] + full[rows:, :rotor] + full[:rows, rotor:]) + full[:rows, :rotor]


def solve_kernel(
    n_row, n_col, stride, counts, source, target_ref, field_hbm, nu_hbm, lower_hbm, diag_hbm,
    out_ref, field, nu, picked, received, arrived, lower, diag, acc, c1_in, c2_src, c2_in, res, part, a_in, b_src, b_in, ysh, yb,
    f_sem, p_sems, w_sem, d_sem, c1_sems, c2_sems, c3_sems, a_sems, b_sems, g_sems,
):
    blocks = diag.shape[0]
    n_quads = n_row // QUAD
    n_x = n_col // CORES
    chunks, chunk_rows, rotor = acc.shape[2:]
    half_rows = chunks * chunk_rows
    chunk_share = diag.shape[1] // n_quads
    r = lax.axis_index("row")
    c = lax.axis_index("col")
    a, b = lax.rem(r, QUAD), lax.div(r, QUAD)
    core = lax.rem(c, CORES)
    other = 1 - core
    core_peer = {"col": c + 1 - 2 * core}
    x_peer = [{"col": lax.rem(c + CORES * s, n_col)} for s in range(1, n_x)]
    a_off = [lax.rem(a + s, QUAD) for s in range(1, QUAD)]
    a_peer = [{"row": b * QUAD + o} for o in a_off]
    b_peer = [{"row": lax.rem(b + s, n_quads) * QUAD + a} for s in range(1, n_quads)]
    row_at = [lax.rem(r + s, n_row) for s in range(n_row)]
    peers = [core_peer] + x_peer + [{"row": g} for g in row_at[1:]]
    slots = source.shape[2]
    strips = [(h, u) for h in range(n_quads) for u in range(SPLIT)]

    def load_lower(k):
        return pltpu.make_async_copy(lower_hbm.at[k], lower.at[k], w_sem.at[k])

    def load_diag(k):
        return pltpu.make_async_copy(diag_hbm.at[k], diag.at[k], d_sem.at[k])

    def load_cells():
        return (
            pltpu.make_async_copy(field_hbm, field, f_sem.at[0]),
            pltpu.make_async_copy(nu_hbm, nu, f_sem.at[1]),
        )

    for copy in load_cells():
        copy.start()
    barrier = pltpu.get_barrier_semaphore()
    for p in peers:
        pl.semaphore_signal(barrier, inc=1, device_id=p, device_id_type=MESH)

    def remote(src, dst, sems, at, device):
        copy = pltpu.make_async_remote_copy(
            src_ref=src, dst_ref=dst, send_sem=sems.at[(0,) + at], recv_sem=sems.at[(1,) + at],
            device_id=device, device_id_type=MESH,
        )
        copy.start()
        return copy

    def finish(copies):
        for copy in copies:
            copy.wait()

    band = stride[0]

    def pick(s):
        g = row_at[s]
        live_slots = counts[0, g]

        def group(k8, carry):
            for u in range(PICKS):
                k = k8 * PICKS + u
                m = source[0, g, k]
                here = field[pl.ds(m, 1), :]
                radial = field[pl.ds(jnp.maximum(m - band, 0), 1), :]
                tangent = field[pl.ds(jnp.maximum(m - 1, 0), 1), :]
                has_radial = jnp.where(m >= band, 1.0, 0.0)
                has_tangent = jnp.where(m >= 1, 1.0, 0.0)
                live = jnp.where(k < live_slots, 1.0, 0.0)
                swept = nu[0, pl.ds(m, 1), :] * (here - radial * has_radial) + nu[
                    1, pl.ds(m, 1), :
                ] * (here - tangent * has_tangent)
                picked[s, pl.ds(k, 1), :] = swept * live
            return carry

        lax.fori_loop(0, slots // PICKS, group, 0)

    for copy in load_cells():
        copy.wait()
    for i in range(blocks):
        load_diag(i).start()
        for j in range(i):
            load_lower(pair_index(i, j)).start()
    sent = []
    for s in range(1, n_row):
        pick(s)
        if s == 1:
            pl.semaphore_wait(barrier, len(peers))
        sent.append(remote(picked.at[s], received.at[r], p_sems, (s - 1,), {"row": row_at[s]}))
    pick(0)
    received[r] = picked[0]
    finish(sent)
    arrived[...] = halves(received[...].reshape(arrived.shape[0], rotor), 1)

    def place(i):
        rows = CORES * half_rows
        here = lax.broadcasted_iota(jnp.int32, (rows, arrived.shape[0]), 0) + i * rows
        chosen = jnp.where(here == target_ref[...], 1.0, 0.0).astype(jnp.bfloat16)
        full = jnp.dot(chosen, arrived[...], preferred_element_type=jnp.float32)
        acc[i] = (full[:, :rotor] + full[:, rotor:]).reshape(acc.shape[1:])

    place(0)

    def lower_step(i, j):
        k = pair_index(i, j)
        load_lower(k).wait()
        product = split_product(lower[k], yb[...])
        acc[i] = acc[i] - product.reshape(acc.shape[1:])

    def lower_half(i, side):
        start = pl.multiple_of(side * half_rows, half_rows)
        product = split_product(lower[pair_index(i, i - 1), pl.ds(start, half_rows)], yb[...])
        acc[i, side] = acc[i, side] - product.reshape(acc.shape[2:])

    def step(i, carry):
        parity = lax.rem(i, 2)

        def deferred(*turns):
            for t in turns:
                @pl.when(jnp.logical_and(i > 0, i + 1 + t < blocks))
                def _():
                    lower_step(i + 1 + t, i - 1)

            @pl.when(i == 0)
            def _():
                for t in turns:
                    if 1 + t < blocks:
                        place(1 + t)

        @pl.when(i > 0)
        def _():
            load_lower(pair_index(i, i - 1)).wait()
            lower_half(i, other)

        c1 = [
            remote(acc.at[i, other, q], c1_in.at[q], c1_sems, (q,), core_peer)
            for q in range(chunks)
        ]

        @pl.when(i > 0)
        def _():
            lower_half(i, core)

        c2 = []
        for q in range(chunks):
            c1[q].wait()
            c2_src[q] = acc[i, core, q] + c1_in[q]
            c2.append([
                remote(c2_src.at[q], c2_in.at[parity, q, s], c2_sems, (parity, q, s), p)
                for s, p in enumerate(x_peer)
            ])
        deferred(0)
        c3 = []
        for q in range(chunks):
            finish(c2[q])
            total = c2_src[q]
            for s in range(n_x - 1):
                total = total + c2_in[parity, q, s]
            res[core, q] = total
            c3.append(remote(res.at[core, q], res.at[core, q], c3_sems, (q,), core_peer))
        load_diag(i).wait()
        finish(c3)

        residual = halves(res[...].reshape(CORES * half_rows, rotor), 1)
        a_copies = []
        for h in range(n_quads):
            rows = diag[i, h * chunk_share:(h + 1) * chunk_share]
            part[h] = split_product(rows, residual).reshape(part.shape[1:])
            a_copies += [
                [
                    remote(part.at[h, o, u], a_in.at[h, u, s], a_sems, (h, u, s), p)
                    for s, (o, p) in enumerate(zip(a_off, a_peer))
                ]
                for u in range(SPLIT)
            ]
        deferred(1, 2)
        b_copies = []
        for n, (h, u) in enumerate(strips):
            finish(a_copies[n])
            total = part[h, a, u]
            for s in range(QUAD - 1):
                total = total + a_in[h, u, s]
            b_src[n] = total
            b_copies.append([
                remote(b_src.at[n], b_in.at[parity, n, s], b_sems, (parity, n, s), p)
                for s, p in enumerate(b_peer)
            ])
        deferred(3)

        def across(n):
            h, u = strips[n]
            finish(b_copies[n])
            total = b_src[n]
            for s in range(n_quads - 1):
                total = total + b_in[parity, n, s]
            ysh[h, a, u] = total

        @pl.when(i < blocks - 1)
        def _():
            back = []
            for n, (h, u) in enumerate(strips):
                across(n)
                back.append([
                    remote(ysh.at[h, a, u], ysh.at[h, a, u], g_sems, (h, u, s), p)
                    for s, p in enumerate(a_peer)
                ])
            deferred(*range(4, blocks - 1))
            for copies in back:
                finish(copies)
            yb[...] = halves(ysh[...].reshape(yb.shape[0], rotor), 1)

        @pl.when(i == blocks - 1)
        def _():
            for n in range(len(strips)):
                across(n)

        out_ref[i] = ysh[b, a].reshape(out_ref.shape[1:])
        return carry

    lax.fori_loop(0, blocks, step, 0)


def per_device(
    sub_field, reluctivity, stride, counts, source_cell, target_row, lower_tiles, diag_inverse
):
    n_row, n_col = lax.axis_size("row"), lax.axis_size("col")
    blocks, tile_rows, rotor = diag_inverse.shape[0], lower_tiles.shape[1], sub_field.shape[1]
    cap = source_cell.shape[2]
    pairs = lower_tiles.shape[0]
    share = diag_inverse.shape[1]
    piece = share // n_row
    quads = n_row // QUAD
    n_x = n_col // CORES
    chunks = 4
    col_chunk = (chunks, tile_rows // CORES // chunks, rotor)
    strip = (piece // SPLIT, rotor)
    f32 = jnp.float32
    vmem = pl.BlockSpec(memory_space=pltpu.VMEM)
    smem = pl.BlockSpec(memory_space=pltpu.SMEM)
    hbm = pl.BlockSpec(memory_space=pl.ANY)
    dma = pltpu.SemaphoreType.DMA
    pieces = pl.pallas_call(
        functools.partial(solve_kernel, n_row, n_col),
        out_shape=jax.ShapeDtypeStruct((blocks, piece, rotor), f32),
        in_specs=[smem, smem, smem, vmem, hbm, hbm, hbm, hbm],
        out_specs=vmem,
        scratch_shapes=[
            pltpu.VMEM(sub_field.shape, f32),
            pltpu.VMEM(reluctivity.shape, f32),
            pltpu.VMEM((n_row, cap, rotor), f32),
            pltpu.VMEM((n_row, cap, rotor), f32),
            pltpu.VMEM((n_row * cap, 2 * rotor), jnp.bfloat16),
            pltpu.VMEM(lower_tiles.shape, f32),
            pltpu.VMEM(diag_inverse.shape, f32),
            pltpu.VMEM((blocks, CORES) + col_chunk, f32),
            pltpu.VMEM(col_chunk, f32),
            pltpu.VMEM(col_chunk, f32),
            pltpu.VMEM((2, chunks, n_x - 1) + col_chunk[1:], f32),
            pltpu.VMEM((CORES,) + col_chunk, f32),
            pltpu.VMEM((quads, QUAD, SPLIT) + strip, f32),
            pltpu.VMEM((quads, SPLIT, QUAD - 1) + strip, f32),
            pltpu.VMEM((quads * SPLIT,) + strip, f32),
            pltpu.VMEM((2, quads * SPLIT, quads - 1) + strip, f32),
            pltpu.VMEM((quads, QUAD, SPLIT) + strip, f32),
            pltpu.VMEM((share, 2 * rotor), jnp.bfloat16),
            dma((2,)),
            dma((2, n_row - 1)),
            dma((pairs,)),
            dma((blocks,)),
            dma((2, chunks)),
            dma((2, 2, chunks, n_x - 1)),
            dma((2, chunks)),
            dma((2, quads, SPLIT, QUAD - 1)),
            dma((2, 2, quads * SPLIT, quads - 1)),
            dma((2, quads, SPLIT, QUAD - 1)),
        ],
        compiler_params=pltpu.CompilerParams(
            collective_id=0, has_side_effects=True, vmem_limit_bytes=48 * 1024 * 1024
        ),
    )(
        stride, counts, source_cell, target_row.reshape(1, n_row * cap),
        sub_field, reluctivity, lower_tiles, diag_inverse,
    )
    return pieces[:, None]


def solution(mesh):
    placed = (
        P(("row", "col"), None),
        P(None, ("row", "col"), None),
        P(("row", "col")),
        P(("row", "col"), None),
        P(("row", "col"), None, None),
        P("row", "col", None, None),
        P(None, "row", "col"),
        P(None, "col", "row"),
    )
    return jax.shard_map(
        per_device,
        mesh=mesh,
        in_specs=placed,
        out_specs=P(None, "col", "row", None),
        check_vma=False,
    )
```

```python
import functools

import jax
import jax.numpy as jnp
from jax import lax
from jax.experimental import pallas as pl
from jax.experimental.pallas import tpu as pltpu
from jax.sharding import PartitionSpec as P

MESH = pl.DeviceIdType.MESH
QUAD = 4
CORES = 2
PICKS = 8
SPLIT = 2


def pair_index(later_block, earlier_block):
    return later_block * (later_block - 1) // 2 + earlier_block


def halves(value, axis):
    high = value.astype(jnp.bfloat16)
    low = (value - high.astype(jnp.float32)).astype(jnp.bfloat16)
    return jnp.concatenate([high, low], axis=axis)


def split_product(left, right_halves):
    rows, rotor = left.shape[0], right_halves.shape[1] // 2
    full = jnp.dot(halves(left, 0), right_halves, preferred_element_type=jnp.float32)
    return (full[rows:, rotor:] + full[rows:, :rotor] + full[:rows, rotor:]) + full[:rows, :rotor]


def solve_kernel(
    n_row, n_col, stride, counts_hbm, source_hbm, target_hbm, field_hbm, nu_hbm, lower_hbm,
    diag_hbm, out_ref, counts, source, target_rows, field, nu, picked, received, arrived, lower, diag, acc, c1_in, c2_src, c2_in, res, part, a_in, b_src, b_in, ysh, yb,
    f_sem, p_sems, w_sem, d_sem, c1_sems, c2_sems, c3_sems, a_sems, b_sems, g_sems,
):
    blocks = diag.shape[0]
    n_quads = n_row // QUAD
    n_x = n_col // CORES
    chunks, chunk_rows, rotor = acc.shape[2:]
    half_rows = chunks * chunk_rows
    chunk_share = diag.shape[1] // n_quads
    r = lax.axis_index("row")
    c = lax.axis_index("col")
    a, b = lax.rem(r, QUAD), lax.div(r, QUAD)
    core = lax.rem(c, CORES)
    other = 1 - core
    core_peer = {"col": c + 1 - 2 * core}
    x_peer = [{"col": lax.rem(c + CORES * s, n_col)} for s in range(1, n_x)]
    a_off = [lax.rem(a + s, QUAD) for s in range(1, QUAD)]
    a_peer = [{"row": b * QUAD + o} for o in a_off]
    b_peer = [{"row": lax.rem(b + s, n_quads) * QUAD + a} for s in range(1, n_quads)]
    row_at = [lax.rem(r + s, n_row) for s in range(n_row)]
    peers = [core_peer] + x_peer + [{"row": g} for g in row_at[1:]]
    slots = source.shape[2]
    strips = [(h, u) for h in range(n_quads) for u in range(SPLIT)]

    def load_lower(k):
        return pltpu.make_async_copy(lower_hbm.at[k], lower.at[k], w_sem.at[k])

    def load_diag(k):
        return pltpu.make_async_copy(diag_hbm.at[k], diag.at[k], d_sem.at[k])

    def load_cells():
        return (
            pltpu.make_async_copy(counts_hbm, counts, f_sem.at[3]),
            pltpu.make_async_copy(source_hbm, source, f_sem.at[4]),
            pltpu.make_async_copy(target_hbm.at[0, 0], target_rows, f_sem.at[2]),
            pltpu.make_async_copy(field_hbm, field, f_sem.at[0]),
            pltpu.make_async_copy(nu_hbm, nu, f_sem.at[1]),
        )

    for copy in load_cells():
        copy.start()
    barrier = pltpu.get_barrier_semaphore()
    for p in peers:
        pl.semaphore_signal(barrier, inc=1, device_id=p, device_id_type=MESH)

    def remote(src, dst, sems, at, device):
        copy = pltpu.make_async_remote_copy(
            src_ref=src, dst_ref=dst, send_sem=sems.at[(0,) + at], recv_sem=sems.at[(1,) + at],
            device_id=device, device_id_type=MESH,
        )
        copy.start()
        return copy

    def finish(copies):
        for copy in copies:
            copy.wait()

    def pick(s):
        g = row_at[s]
        band = stride[0]
        live_slots = counts[0, g]

        def group(k8, carry):
            for u in range(PICKS):
                k = k8 * PICKS + u
                m = source[0, g, k]
                here = field[pl.ds(m, 1), :]
                radial = field[pl.ds(jnp.maximum(m - band, 0), 1), :]
                tangent = field[pl.ds(jnp.maximum(m - 1, 0), 1), :]
                has_radial = jnp.where(m >= band, 1.0, 0.0)
                has_tangent = jnp.where(m >= 1, 1.0, 0.0)
                live = jnp.where(k < live_slots, 1.0, 0.0)
                swept = nu[0, pl.ds(m, 1), :] * (here - radial * has_radial) + nu[
                    1, pl.ds(m, 1), :
                ] * (here - tangent * has_tangent)
                picked[s, pl.ds(k, 1), :] = swept * live
            return carry

        lax.fori_loop(0, slots // PICKS, group, 0)

    for copy in load_cells():
        copy.wait()
    for i in range(blocks):
        load_diag(i).start()
        for j in range(i):
            load_lower(pair_index(i, j)).start()
    sent = []
    for s in range(1, n_row):
        pick(s)
        if s == 1:
            pl.semaphore_wait(barrier, len(peers))
        sent.append(remote(picked.at[s], received.at[r], p_sems, (s - 1,), {"row": row_at[s]}))
    pick(0)
    received[r] = picked[0]
    finish(sent)
    arrived[...] = halves(received[...].reshape(arrived.shape[0], rotor), 1)

    targets = jnp.concatenate([target_rows[q:q + 1, :] for q in range(n_row)], axis=1)

    def place(i):
        rows = CORES * half_rows
        here = lax.broadcasted_iota(jnp.int32, (rows, arrived.shape[0]), 0) + i * rows
        chosen = jnp.where(here == targets, 1.0, 0.0).astype(jnp.bfloat16)
        full = jnp.dot(chosen, arrived[...], preferred_element_type=jnp.float32)
        acc[i] = (full[:, :rotor] + full[:, rotor:]).reshape(acc.shape[1:])

    place(0)

    def lower_step(i, j):
        k = pair_index(i, j)
        load_lower(k).wait()
        product = split_product(lower[k], yb[...])
        acc[i] = acc[i] - product.reshape(acc.shape[1:])

    def lower_half(i, side):
        start = pl.multiple_of(side * half_rows, half_rows)
        product = split_product(lower[pair_index(i, i - 1), pl.ds(start, half_rows)], yb[...])
        acc[i, side] = acc[i, side] - product.reshape(acc.shape[2:])

    def step(i, carry):
        parity = lax.rem(i, 2)

        def deferred(*turns):
            for t in turns:
                @pl.when(jnp.logical_and(i > 0, i + 1 + t < blocks))
                def _():
                    lower_step(i + 1 + t, i - 1)

            @pl.when(i == 0)
            def _():
                for t in turns:
                    if 1 + t < blocks:
                        place(1 + t)

        @pl.when(i > 0)
        def _():
            load_lower(pair_index(i, i - 1)).wait()
            lower_half(i, other)

        c1 = [
            remote(acc.at[i, other, q], c1_in.at[q], c1_sems, (q,), core_peer)
            for q in range(chunks)
        ]

        @pl.when(i > 0)
        def _():
            lower_half(i, core)

        c2 = []
        for q in range(chunks):
            c1[q].wait()
            c2_src[q] = acc[i, core, q] + c1_in[q]
            c2.append([
                remote(c2_src.at[q], c2_in.at[parity, q, s], c2_sems, (parity, q, s), p)
                for s, p in enumerate(x_peer)
            ])
        deferred(0)
        c3 = []
        for q in range(chunks):
            finish(c2[q])
            total = c2_src[q]
            for s in range(n_x - 1):
                total = total + c2_in[parity, q, s]
            res[core, q] = total
            c3.append(remote(res.at[core, q], res.at[core, q], c3_sems, (q,), core_peer))
        load_diag(i).wait()
        finish(c3)

        residual = halves(res[...].reshape(CORES * half_rows, rotor), 1)
        a_copies = []
        for h in range(n_quads):
            rows = diag[i, h * chunk_share:(h + 1) * chunk_share]
            part[h] = split_product(rows, residual).reshape(part.shape[1:])
            a_copies += [
                [
                    remote(part.at[h, o, u], a_in.at[h, u, s], a_sems, (h, u, s), p)
                    for s, (o, p) in enumerate(zip(a_off, a_peer))
                ]
                for u in range(SPLIT)
            ]
        deferred(1, 2)
        b_copies = []
        for n, (h, u) in enumerate(strips):
            finish(a_copies[n])
            total = part[h, a, u]
            for s in range(QUAD - 1):
                total = total + a_in[h, u, s]
            b_src[n] = total
            b_copies.append([
                remote(b_src.at[n], b_in.at[parity, n, s], b_sems, (parity, n, s), p)
                for s, p in enumerate(b_peer)
            ])
        deferred(3)

        def across(n):
            h, u = strips[n]
            finish(b_copies[n])
            total = b_src[n]
            for s in range(n_quads - 1):
                total = total + b_in[parity, n, s]
            ysh[h, a, u] = total

        @pl.when(i < blocks - 1)
        def _():
            back = []
            for n, (h, u) in enumerate(strips):
                across(n)
                back.append([
                    remote(ysh.at[h, a, u], ysh.at[h, a, u], g_sems, (h, u, s), p)
                    for s, p in enumerate(a_peer)
                ])
            deferred(*range(4, blocks - 1))
            for copies in back:
                finish(copies)
            yb[...] = halves(ysh[...].reshape(yb.shape[0], rotor), 1)

        @pl.when(i == blocks - 1)
        def _():
            for n in range(len(strips)):
                across(n)

        out_ref[i] = ysh[b, a].reshape(out_ref.shape[1:])
        return carry

    lax.fori_loop(0, blocks, step, 0)


def per_device(
    sub_field, reluctivity, stride, counts, source_cell, target_row, lower_tiles, diag_inverse
):
    n_row, n_col = lax.axis_size("row"), lax.axis_size("col")
    blocks, tile_rows, rotor = diag_inverse.shape[0], lower_tiles.shape[1], sub_field.shape[1]
    cap = source_cell.shape[2]
    pairs = lower_tiles.shape[0]
    share = diag_inverse.shape[1]
    piece = share // n_row
    quads = n_row // QUAD
    n_x = n_col // CORES
    chunks = 4
    col_chunk = (chunks, tile_rows // CORES // chunks, rotor)
    strip = (piece // SPLIT, rotor)
    f32 = jnp.float32
    vmem = pl.BlockSpec(memory_space=pltpu.VMEM)
    hbm = pl.BlockSpec(memory_space=pltpu.HBM)
    dma = pltpu.SemaphoreType.DMA
    pieces = pl.pallas_call(
        functools.partial(solve_kernel, n_row, n_col),
        out_shape=jax.ShapeDtypeStruct((blocks, piece, rotor), f32),
        in_specs=[pl.BlockSpec(memory_space=pltpu.SMEM)] + [hbm] * 7,
        out_specs=vmem,
        scratch_shapes=[
            pltpu.SMEM(counts.shape, jnp.int32),
            pltpu.SMEM(source_cell.shape, jnp.int32),
            pltpu.VMEM((n_row, cap), jnp.int32),
            pltpu.VMEM(sub_field.shape, f32),
            pltpu.VMEM(reluctivity.shape, f32),
            pltpu.VMEM((n_row, cap, rotor), f32),
            pltpu.VMEM((n_row, cap, rotor), f32),
            pltpu.VMEM((n_row * cap, 2 * rotor), jnp.bfloat16),
            pltpu.VMEM(lower_tiles.shape, f32),
            pltpu.VMEM(diag_inverse.shape, f32),
            pltpu.VMEM((blocks, CORES) + col_chunk, f32),
            pltpu.VMEM(col_chunk, f32),
            pltpu.VMEM(col_chunk, f32),
            pltpu.VMEM((2, chunks, n_x - 1) + col_chunk[1:], f32),
            pltpu.VMEM((CORES,) + col_chunk, f32),
            pltpu.VMEM((quads, QUAD, SPLIT) + strip, f32),
            pltpu.VMEM((quads, SPLIT, QUAD - 1) + strip, f32),
            pltpu.VMEM((quads * SPLIT,) + strip, f32),
            pltpu.VMEM((2, quads * SPLIT, quads - 1) + strip, f32),
            pltpu.VMEM((quads, QUAD, SPLIT) + strip, f32),
            pltpu.VMEM((share, 2 * rotor), jnp.bfloat16),
            dma((5,)),
            dma((2, n_row - 1)),
            dma((pairs,)),
            dma((blocks,)),
            dma((2, chunks)),
            dma((2, 2, chunks, n_x - 1)),
            dma((2, chunks)),
            dma((2, quads, SPLIT, QUAD - 1)),
            dma((2, 2, quads * SPLIT, quads - 1)),
            dma((2, quads, SPLIT, QUAD - 1)),
        ],
        compiler_params=pltpu.CompilerParams(
            collective_id=0, has_side_effects=True, vmem_limit_bytes=67043328
        ),
    )(
        stride, counts, source_cell, target_row, sub_field, reluctivity, lower_tiles, diag_inverse
    )
    return pieces[:, None]


def solution(mesh):
    placed = (
        P(("row", "col"), None),
        P(None, ("row", "col"), None),
        P(("row", "col")),
        P(("row", "col"), None),
        P(("row", "col"), None, None),
        P("row", "col", None, None),
        P(None, "row", "col"),
        P(None, "col", "row"),
    )
    return jax.shard_map(
        per_device,
        mesh=mesh,
        in_specs=placed,
        out_specs=P(None, "col", "row", None),
        check_vma=False,
    )
```
